32 devices in a mesh: mod: 4 (over z), frm: 2 (over x), ori: 4 (over y, core).
Axes of the slice: x: 2, y: 2, z: 4, core: 2. Of those that a mesh axis runs over, the one named last changes fastest.
Arguments:
- counts: int32 [512, 128, 128], P(('frm', 'ori'), 'mod'), may hold values from 0 to 8
- slice_codes: int32 [4096, 128, 128], P('ori', ('mod', 'frm')), may hold values from 0 to 2047
- pixel_mask: int32 [128, 128], P('mod'), may hold values 0 or 1
Outputs:
- log_posterior: float32 [2, 256, 4096], P('frm', 'mod', 'ori')
The draws below stay inside these ranges and needn't reach their ends.
All inputs are finite; a program needn't handle non-finite values. No bound on the sum of `pixel_mask` on one device may be relied on, other than what follows from the above.
Results may differ from the reference program's by a relative error of at most 0.0024.
Values may be sent and summed in bfloat16 or wider, within the bound.
A program may use at most 64 MiB of HBM per device.

```python
import math
import jax
import jax.numpy as jnp
from jax import lax

MCOLS = 128
ORIENT = 4096
PASSES = 8
FR_DEV = 64
ROWS = 128
FRAMES = 512
N_FRM = 2
N_ORI = 4


def draw_counts(key, part):
    level_key, pick_key, count_key = jax.random.split(key, 3)
    levels = jax.random.randint(level_key, (FRAMES,), 1, 9)
    brightest = jax.random.randint(pick_key, (), 0, FRAMES)
    levels = jnp.where(jnp.arange(FRAMES) == brightest, 8, levels)
    raw_values = jax.random.randint(count_key, (FRAMES, ROWS, MCOLS), 0, 65536)
    return (raw_values % (levels[:, None, None] + 1)).astype(jnp.int32)


def plant(array, stream_key, least, largest):
    index_at = [jax.random.randint(jax.random.fold_in(stream_key, axis), (), 0, length) for axis, length in enumerate(array.shape)]
    longest = array.shape.index(max(array.shape))
    next_to = index_at[:longest] + [(index_at[longest] + 1) % array.shape[longest]] + index_at[longest + 1:]
    return array.at[tuple(index_at)].set(least).at[tuple(next_to)].set(largest)


def setup_inputs(seed: int = 0) -> dict:
    key_of = jax.random.split(jax.random.key(seed), 4)
    return {
        "counts": draw_counts(jax.random.fold_in(key_of[3], 71), 0),
        "slice_codes": plant(jax.random.randint(key_of[1], (ORIENT, ROWS, MCOLS), 0, 2048), jax.random.fold_in(key_of[1], 1), 0, 2047).astype(jnp.int32),
        "pixel_mask": plant((jax.random.randint(key_of[2], (ROWS, MCOLS), 0, 16) < 15).astype(jnp.int32), jax.random.fold_in(key_of[2], 1), 0, 1),
    }


TIME_STEP = 0.2
EDGE_SCALE = 2.0
LOG_FLOOR = -7.0
CODE_STEP = 1.0 / 256.0

def conduct(difference):
    ratio = difference / EDGE_SCALE
    return difference / (1.0 + ratio * ratio)

def diffuse(frames):
    intensity = frames.astype(jnp.float32)
    for sweep_index in range(PASSES):
        padded = jnp.pad(intensity, ((0, 0), (1, 1), (1, 1)))
        centre = padded[:, 1:-1, 1:-1]
        flux_sum = conduct(padded[:, :-2, 1:-1] - centre) + conduct(padded[:, 2:, 1:-1] - centre)
        flux_sum = flux_sum + conduct(padded[:, 1:-1, :-2] - centre) + conduct(padded[:, 1:-1, 2:] - centre)
        intensity = centre + TIME_STEP * flux_sum
    return intensity.astype(jnp.bfloat16)

def reference(counts, slice_codes, pixel_mask):
    blocks = counts.reshape(FRAMES // FR_DEV, FR_DEV, ROWS, MCOLS)
    cleaned = lax.map(diffuse, blocks).reshape(FRAMES, ROWS * MCOLS)
    weights = pixel_mask.reshape(ROWS * MCOLS)
    masked = cleaned * weights.astype(jnp.bfloat16)[None, :]
    mask_float = weights.astype(jnp.float32)
    block_size = ORIENT // N_ORI

    def orient_block(codes):
        log_slices = (LOG_FLOOR + codes.astype(jnp.float32) * CODE_STEP).astype(jnp.bfloat16)
        log_slices = log_slices.reshape(block_size, ROWS * MCOLS)
        totals = lax.optimization_barrier(jnp.sum(jnp.exp(log_slices.astype(jnp.float32)) * mask_float[None, :], axis=1))
        cross_terms = jnp.dot(masked, log_slices.T, preferred_element_type=jnp.float32)
        return cross_terms - totals[None, :]
    parts = lax.map(orient_block, slice_codes.reshape(N_ORI, block_size, ROWS, MCOLS))
    scores = jnp.transpose(parts, (1, 0, 2)).reshape(FRAMES, ORIENT) * (1.0 / math.sqrt(ROWS * MCOLS))
    peaks = lax.optimization_barrier(jnp.max(scores, axis=1, keepdims=True))
    masses = lax.optimization_barrier(jnp.sum(jnp.exp(scores - peaks), axis=1, keepdims=True))
    log_posterior = scores - (peaks + jnp.log(masses))
    return log_posterior.reshape(N_FRM, FRAMES // N_FRM, ORIENT)
```

```python
import functools
import math

import jax
import jax.numpy as jnp
from jax import lax
from jax.experimental import pallas as pl
from jax.experimental.pallas import tpu as pltpu
from jax.sharding import PartitionSpec as P

PASSES = 8
TIME_STEP = 0.2
EDGE_SCALE = 2.0
LOG_FLOOR = -7.0
CODE_STEP = 1.0 / 256.0
GROUPS = 2
STRIDE_ROWS = 8
SLICE_CHUNK = 128
MESH = pl.DeviceIdType.MESH


SQUARE = EDGE_SCALE * EDGE_SCALE
DENOM = 1.0 / TIME_STEP
SCALE = math.sqrt(DENOM / SQUARE)
TILE = 256


def flux(v):
    return v / (DENOM + v * v)


def flip(h, b):
    return h + b - 2 * b * lax.rem(h // b, 2)


def group_count(nm, no, fr):
    count = 4
    while count > 1 and (nm > no or no % nm or fr % (16 * count)):
        count //= 2
    return count


def kernel(
    dims, counts, codes, mask, out,
    codes_v, logs, inten, halo_s, halo_r, band_s, frames, cross, centre, xs, xr, zs, zr,
    score, stat_s, stat_r, totals,
    code_sem, hs_sem, hr_sem, own_sem, gs_sem, gr_sem, xs_sem, xr_sem, zs_sem, zr_sem,
    ts_sem, tr_sem,
):
    nm, nf, no, fr, rows, orient, band, groups = dims
    m, f, o = lax.axis_index("mod"), lax.axis_index("frm"), lax.axis_index("ori")
    sizes = {"mod": (m, nm), "frm": (f, nf), "ori": (o, no)}
    lanes = counts.shape[1]
    high = rows + 2 * PASSES
    gsz = fr // groups
    gg = no * gsz
    sg = gg // nm
    chunks = orient // SLICE_CHUNK
    tiles = orient // TILE
    f32, bf16 = jnp.float32, jnp.bfloat16

    def other(axis, d):
        me, n = sizes[axis]
        return lax.rem(me + d, n)

    def code_copy(c):
        span = SLICE_CHUNK * band
        at = pl.ds(c * span, span)
        return pltpu.make_async_copy(codes.at[at], codes_v.at[at], code_sem.at[c])

    for c in range(chunks):
        code_copy(c).start()

    barrier = pltpu.get_barrier_semaphore()
    for axis in ("mod", "frm", "ori"):
        for d in range(1, sizes[axis][1]):
            pl.semaphore_signal(
                barrier, inc=1, device_id={axis: other(axis, d)}, device_id_type=MESH
            )

    def count_row(i):
        return counts[pl.ds(i, fr, stride=rows), :].astype(f32)

    for i in range(PASSES):
        halo_s[0, i] = count_row(i).astype(bf16)
        halo_s[1, i] = count_row(rows - PASSES + i).astype(bf16)
    pl.semaphore_wait(barrier, nm + nf + no - 3)

    first, last = m == 0, m == nm - 1

    def part(g):
        return pl.ds(g * gsz, gsz)

    def halo_copy(side, g):
        return pltpu.make_async_remote_copy(
            src_ref=halo_s.at[side, :, part(g), :],
            dst_ref=halo_r.at[1 - side, :, part(g), :],
            send_sem=hs_sem.at[side, g],
            recv_sem=hr_sem.at[1 - side, g],
            device_id={"mod": other("mod", nm - 1 if side == 0 else 1)},
            device_id_type=MESH,
        )

    @pl.when(jnp.logical_not(first))
    def _():
        for g in range(groups):
            halo_copy(0, g).start()

    @pl.when(jnp.logical_not(last))
    def _():
        for g in range(groups):
            halo_copy(1, g).start()

    def load_row(i, carry):
        inten[PASSES + i] = count_row(i) * SCALE
        return carry

    lax.fori_loop(0, rows, load_row, 0)
    inten[pl.ds(high, STRIDE_ROWS)] = jnp.zeros((STRIDE_ROWS, fr, lanes), f32)

    def slice_chunk(c):
        code_copy(c).wait()
        base = c * (SLICE_CHUNK * band)
        acc = jnp.zeros((SLICE_CHUNK, lanes), f32)
        for s in range(band):
            raw = codes_v[pl.ds(base + s, SLICE_CHUNK, stride=band), :]
            value = (LOG_FLOOR + raw.astype(f32) * CODE_STEP).astype(bf16)
            logs[pl.ds(c * SLICE_CHUNK, SLICE_CHUNK), pl.ds(s * lanes, lanes)] = value
            weight = mask[pl.ds(f * band + s, 1), :].astype(f32)
            acc = acc + jnp.exp(value.astype(f32)) * weight
        totals[:, pl.ds(c * SLICE_CHUNK, SLICE_CHUNK)] = jnp.sum(acc.T, axis=0, keepdims=True)

    def halo_in(g):
        @pl.when(first)
        def _():
            inten[pl.ds(0, PASSES), part(g), :] = jnp.zeros((PASSES, gsz, lanes), f32)

        @pl.when(jnp.logical_not(first))
        def _():
            halo_copy(1, g).wait_recv()
            inten[pl.ds(0, PASSES), part(g), :] = halo_r[0, :, part(g), :].astype(f32) * SCALE
            halo_copy(0, g).wait_send()

        @pl.when(last)
        def _():
            inten[pl.ds(PASSES + rows, PASSES), part(g), :] = jnp.zeros((PASSES, gsz, lanes), f32)

        @pl.when(jnp.logical_not(last))
        def _():
            halo_copy(0, g).wait_recv()
            inten[pl.ds(PASSES + rows, PASSES), part(g), :] = (
                halo_r[1, :, part(g), :].astype(f32) * SCALE
            )
            halo_copy(1, g).wait_send()

    lane = lax.broadcasted_iota(jnp.int32, (gsz, lanes), 1)
    at_left, at_right = lane == 0, lane == lanes - 1

    def diffuse(g):
        halo_in(g)
        at = part(g)

        def one_pass(p, carry):
            low = jnp.where(first, PASSES, p + 1)
            top = jnp.where(last, PASSES + rows, high - 1 - p)
            c = inten[low, at, :]
            before = flux(c - inten[low - 1, at, :])

            def some_rows(k, state):
                c, before = state
                i = low + STRIDE_ROWS * k
                below = [inten[i + r + 1, at, :] for r in range(STRIDE_ROWS)]
                fresh = []
                for r in range(STRIDE_ROWS):
                    after = flux(below[r] - c)
                    right = jnp.where(at_right, 0.0, pltpu.roll(c, lanes - 1, 1))
                    east = flux(right - c)
                    west = jnp.where(at_left, flux(c), pltpu.roll(east, 1, 1))
                    fresh.append(c + ((after - before) + (east - west)))
                    c, before = below[r], after
                for r in range(STRIDE_ROWS):
                    inten[i + r, at, :] = fresh[r]
                return c, before

            trips = (top - low + STRIDE_ROWS - 1) // STRIDE_ROWS
            lax.fori_loop(0, trips, some_rows, (c, before))
            edge = inten[PASSES + rows, at, :]
            inten[PASSES + rows, at, :] = jnp.where(last, 0.0, edge)
            return carry

        lax.fori_loop(0, PASSES, one_pass, 0)
        for i in range(rows):
            good = mask[i : i + 1, :].astype(f32) * (1.0 / SCALE)
            band_s[
                pl.ds((i // band) * fr + g * gsz, gsz), pl.ds((i % band) * lanes, lanes)
            ] = (inten[PASSES + i, at, :] * good).astype(bf16)

    def slot(ff, oo, g):
        return frames.at[pl.ds(((g * nf + ff) * no + oo) * gsz, gsz)]

    pending = []
    count = [0]

    def arrived(ff, oo, g):
        pltpu.make_async_remote_copy(
            src_ref=slot(ff, oo, g), dst_ref=slot(ff, oo, g),
            send_sem=gs_sem.at[0], recv_sem=gr_sem.at[ff * no + oo, g],
            device_id={"ori": other("ori", 1)}, device_id_type=MESH,
        ).wait_recv()

    def send(src, ff, oo, g, target):
        copy = pltpu.make_async_remote_copy(
            src_ref=src, dst_ref=slot(ff, oo, g),
            send_sem=gs_sem.at[count[0]], recv_sem=gr_sem.at[ff * no + oo, g],
            device_id=target, device_id_type=MESH,
        )
        count[0] += 1
        copy.start()
        pending.append(copy)

    def banded(ff, g):
        return band_s.at[pl.ds(ff * fr + g * gsz, gsz)]

    bits = []
    b = no // 2
    while b >= 1:
        bits.append(b)
        b //= 2
    hops = len(bits)

    held = [[o]]
    for b in bits:
        held.append(held[-1] + [flip(h, b) for h in held[-1]])

    def first_hop(g):
        for d in range(1, nf):
            fd = other("frm", d)
            send(banded(fd, g), f, o, g, {"frm": fd})
        send(banded(f, g), f, o, g, {"ori": flip(o, bits[0])})
        own = pltpu.make_async_copy(banded(f, g), slot(f, o, g), own_sem.at[g])
        own.start()
        own.wait()

    def second_hop(g):
        for d in range(1, nf):
            fd = other("frm", d)
            arrived(fd, o, g)
            send(slot(fd, o, g), fd, o, g, {"ori": flip(o, bits[0])})

    def later_hop(k, g):
        for d in range(nf):
            for h in held[k][len(held[k]) // 2 :]:
                arrived(other("frm", d), h, g)
        if k < hops:
            for d in range(nf):
                for h in held[k]:
                    send(slot(other("frm", d), h, g), other("frm", d), h, g, {"ori": flip(o, bits[k])})

    def mine(ff):
        return pl.ds(pl.multiple_of(ff * gg, gg), gg)

    def columns(t):
        return pl.ds(t * TILE, TILE)

    def sent_columns(t):
        return pl.ds(0, lanes + TILE) if t == 0 else pl.ds(lanes + t * TILE, TILE)

    def x_copy(src_f, dst_f, g, t, n):
        return pltpu.make_async_remote_copy(
            src_ref=xs.at[g, dst_f, :, sent_columns(t)],
            dst_ref=xr.at[g, src_f, :, sent_columns(t)],
            send_sem=xs_sem.at[g, n, t], recv_sem=xr_sem.at[g, src_f, t],
            device_id={"frm": dst_f}, device_id_type=MESH,
        )

    def multiply(g, t):
        value = lax.dot_general(
            frames[pl.ds(g * nf * gg, nf * gg), :],
            logs[columns(t), :],
            (((1,), (1,)), ((), ())),
            preferred_element_type=f32,
        ) - totals[:, columns(t)]
        cross[g, :, columns(t)] = value
        if t == 0:
            mean = jnp.mean(value, axis=1, keepdims=True).astype(bf16).astype(f32)
            centre[g] = jnp.broadcast_to(mean, (nf * gg, lanes))
        for d in range(1, nf):
            fd = other("frm", d)
            middle = centre[g, mine(fd), :]
            if t == 0:
                xs[g, fd, :, pl.ds(0, lanes)] = middle.astype(bf16)
            for j in range(TILE // lanes):
                at = t * TILE + j * lanes
                xs[g, fd, :, pl.ds(lanes + at, lanes)] = (
                    cross[g, mine(fd), pl.ds(at, lanes)] - middle
                ).astype(bf16)
            copy = x_copy(f, fd, g, t, d)
            copy.start()
            pending.append(copy)

    def z_copy(src_m, dst_m, g, t, n):
        return pltpu.make_async_remote_copy(
            src_ref=zs.at[g, pl.ds(pl.multiple_of(dst_m * sg, sg), sg), sent_columns(t)],
            dst_ref=zr.at[g, src_m, :, sent_columns(t)],
            send_sem=zs_sem.at[g, n, t], recv_sem=zr_sem.at[g, src_m, t],
            device_id={"mod": dst_m}, device_id_type=MESH,
        )

    def reduce_frm(g, t):
        for d in range(1, nf):
            fd = other("frm", d)
            x_copy(fd, f, g, t, 0).wait_recv()
        parts = [(xr, other("frm", d)) for d in range(1, nf)]
        mids = [r[g, i, :, pl.ds(0, lanes)].astype(f32) for r, i in parts]
        middle = sum(mids, centre[g, mine(f), :]).astype(bf16).astype(f32)
        if t == 0:
            zs[g, :, pl.ds(0, lanes)] = middle.astype(bf16)
        for j in range(TILE // lanes):
            at = t * TILE + j * lanes
            value = cross[g, mine(f), pl.ds(at, lanes)]
            for (r, i), mid in zip(parts, mids):
                value = value + (r[g, i, :, pl.ds(lanes + at, lanes)].astype(f32) + mid)
            cross[g, mine(f), pl.ds(at, lanes)] = value
            zs[g, :, pl.ds(lanes + at, lanes)] = (value - middle).astype(bf16)
        for d in range(1, nm):
            copy = z_copy(m, other("mod", d), g, t, d)
            copy.start()
            pending.append(copy)

    wide = lax.broadcasted_iota(jnp.int32, (sg, 128), 1)

    def t_copy(src_o, dst_o, g, n):
        return pltpu.make_async_remote_copy(
            src_ref=stat_s.at[g], dst_ref=stat_r.at[g, src_o],
            send_sem=ts_sem.at[g, n], recv_sem=tr_sem.at[g, src_o],
            device_id={"ori": dst_o}, device_id_type=MESH,
        )

    def reduce_mod(g):
        for t in range(tiles):
            for d in range(1, nm):
                z_copy(other("mod", d), m, g, t, 0).wait_recv()
        at = pl.ds(pl.multiple_of(f * gg + m * sg, sg), sg)
        value = cross[g, at, :]
        for d in range(1, nm):
            md = other("mod", d)
            value = value + (
                zr[g, md, :, pl.ds(lanes, orient)].astype(f32) + zr[g, md, :, pl.ds(0, 1)].astype(f32)
            )
        value = value * (1.0 / math.sqrt(rows * nm * lanes))
        score[g] = value
        peak = jnp.max(value, axis=1, keepdims=True)
        mass = jnp.sum(jnp.exp(value - peak), axis=1, keepdims=True)
        stat_s[g] = jnp.where(wide < 64, peak, mass)
        for d in range(1, no):
            copy = t_copy(o, other("ori", d), g, d)
            copy.start()
            pending.append(copy)

    def finish(g):
        got = [stat_s[g]]
        for d in range(1, no):
            od = other("ori", d)
            t_copy(od, o, g, 0).wait_recv()
            got.append(stat_r[g, od])
        peaks, masses = [s[:, 0:1] for s in got], [s[:, 64:65] for s in got]
        top = functools.reduce(jnp.maximum, peaks)
        weight = sum(s * jnp.exp(p - top) for p, s in zip(peaks, masses))
        value = score[g] - (top + jnp.log(weight))
        blocks = 1 if groups == 1 else no // nm
        span = sg // blocks
        for s in range(blocks):
            out[pl.ds(s * fr + g * gsz, span), :] = value[s * span : (s + 1) * span, :]

    early = chunks // 2
    tasks = []

    def task(when, call, *args):
        tasks.append((when, len(tasks), call, args))

    for c in range(chunks):
        task(-1.0 if c < early else 0.6, slice_chunk, c)
    for g in range(groups):
        task(g, diffuse, g)
        task(g + 0.1, first_hop, g)
        task(g + 1.2, second_hop, g)
        for k in range(1, hops + 1):
            task(g + 1.3 + 0.95 * k, later_hop, k, g)
        for t in range(tiles):
            task(g + 1.4 + 0.95 * hops, multiply, g, t)
        for t in range(tiles):
            task(g + 2.5 + 0.95 * hops, reduce_frm, g, t)
        task(g + 3.6 + 0.95 * hops, reduce_mod, g)
        task(g + 4.7 + 0.95 * hops, finish, g)
    for _, _, call, args in sorted(tasks, key=lambda entry: entry[:2]):
        call(*args)
    for copy in pending:
        copy.wait_send()


def body(counts, slice_codes, pixel_mask):
    nm, nf, no = (lax.axis_size(a) for a in ("mod", "frm", "ori"))
    fr, rows, lanes = counts.shape
    orient, band, _ = slice_codes.shape
    group = no * fr
    share = group // nm
    depth = band * lanes
    high = rows + 2 * PASSES
    groups = group_count(nm, no, fr)
    gg = group // groups
    sg = gg // nm
    tiles = orient // TILE
    dims = (nm, nf, no, fr, rows, orient, band, groups)
    dma = pltpu.SemaphoreType.DMA
    f32, bf16 = jnp.float32, jnp.bfloat16
    vmem = pl.BlockSpec(memory_space=pltpu.VMEM)
    result = pl.pallas_call(
        functools.partial(kernel, dims),
        out_shape=jax.ShapeDtypeStruct((share, orient), f32),
        in_specs=[vmem, pl.BlockSpec(memory_space=pl.ANY), vmem],
        out_specs=vmem,
        scratch_shapes=[
            pltpu.VMEM((orient * band, lanes), jnp.int32),
            pltpu.VMEM((orient, depth), bf16),
            pltpu.VMEM((high + STRIDE_ROWS, fr, lanes), f32),
            pltpu.VMEM((2, PASSES, fr, lanes), bf16),
            pltpu.VMEM((2, PASSES, fr, lanes), bf16),
            pltpu.VMEM((nf * fr, depth), bf16),
            pltpu.VMEM((nf * group, depth), bf16),
            pltpu.VMEM((groups, nf * gg, orient), f32),
            pltpu.VMEM((groups, nf * gg, lanes), f32),
            pltpu.VMEM((groups, nf, gg, lanes + orient), bf16),
            pltpu.VMEM((groups, nf, gg, lanes + orient), bf16),
            pltpu.VMEM((groups, gg, lanes + orient), bf16),
            pltpu.VMEM((groups, nm, sg, lanes + orient), bf16),
            pltpu.VMEM((groups, sg, orient), f32),
            pltpu.VMEM((groups, sg, 128), f32),
            pltpu.VMEM((groups, no, sg, 128), f32),
            pltpu.VMEM((1, orient), f32),
            dma((orient // SLICE_CHUNK,)),
            dma((2, groups)),
            dma((2, groups)),
            dma((groups,)),
            dma((groups * nf * (no + 1),)),
            dma((nf * no, groups)),
            dma((groups, nf, tiles)),
            dma((groups, nf, tiles)),
            dma((groups, nm, tiles)),
            dma((groups, nm, tiles)),
            dma((groups, no)),
            dma((groups, no)),
        ],
        compiler_params=pltpu.CompilerParams(collective_id=0, has_side_effects=True),
    )(counts.reshape(fr * rows, lanes), slice_codes.reshape(orient * band, lanes), pixel_mask)
    return result[None]


def solution(mesh):
    in_specs = (P(("frm", "ori"), "mod", None), P("ori", ("mod", "frm"), None), P("mod", None))
    out_specs = P("frm", "mod", "ori")
    return jax.shard_map(body, mesh=mesh, in_specs=in_specs, out_specs=out_specs, check_vma=False)
```

```python
import functools
import math

import jax
import jax.numpy as jnp
from jax import lax
from jax.experimental import pallas as pl
from jax.experimental.pallas import tpu as pltpu
from jax.sharding import PartitionSpec as P

PASSES = 8
TIME_STEP = 0.2
EDGE_SCALE = 2.0
LOG_FLOOR = -7.0
CODE_STEP = 1.0 / 256.0
GROUPS = 2
STRIDE_ROWS = 8
SLICE_CHUNK = 128
MESH = pl.DeviceIdType.MESH


SQUARE = EDGE_SCALE * EDGE_SCALE
DENOM = 1.0 / TIME_STEP
SCALE = math.sqrt(DENOM / SQUARE)
TILE = 256


def flux(v):
    return v / (DENOM + v * v)


def flip(h, b):
    return h + b - 2 * b * lax.rem(h // b, 2)


def group_count(nm, no, fr):
    count = 4
    while count > 1 and (nm > no or no % nm or fr % (16 * count)):
        count //= 2
    return count


def kernel(
    dims, counts_h, codes, mask_h, out,
    counts, mask, codes_v, logs, inten, halo_s, halo_r, band_s, frames, cross, centre, xs, xr, zs, zr,
    score, stat_s, stat_r, totals, split, slope,
    load_sem, know, code_sem, hs_sem, hr_sem, own_sem, gs_sem, gr_sem, xs_sem, xr_sem, zs_sem, zr_sem,
    ts_sem, tr_sem,
):
    nm, nf, no, fr, rows, orient, band, groups = dims
    m, f, o = lax.axis_index("mod"), lax.axis_index("frm"), lax.axis_index("ori")
    sizes = {"mod": (m, nm), "frm": (f, nf), "ori": (o, no)}
    lanes = counts.shape[1]
    high = rows + 2 * PASSES
    gsz = fr // groups
    gg = no * gsz
    sg = gg // nm
    chunks = orient // SLICE_CHUNK
    tiles = orient // TILE
    f32, bf16 = jnp.float32, jnp.bfloat16

    def other(axis, d):
        me, n = sizes[axis]
        return lax.rem(me + d, n)

    def code_copy(c):
        span = SLICE_CHUNK * band
        at = pl.ds(c * span, span)
        return pltpu.make_async_copy(codes.at[at], codes_v.at[at], code_sem.at[c])

    loads = [
        pltpu.make_async_copy(counts_h, counts, load_sem.at[0]),
        pltpu.make_async_copy(mask_h, mask, load_sem.at[1]),
    ]
    for copy in loads:
        copy.start()
    for c in range(chunks):
        code_copy(c).start()

    first, last = m == 0, m == nm - 1
    bits = []
    b = no // 2
    while b >= 1:
        bits.append(b)
        b //= 2
    hops = len(bits)
    links = nf - 1 + hops + jnp.where(first, 0, 1) + jnp.where(last, 0, 1)
    rounds = max(nm - 1, hops) - 1

    def greet(sem):
        def hello(target):
            pl.semaphore_signal(sem, inc=1, device_id=target, device_id_type=MESH)

        @pl.when(jnp.logical_not(first))
        def _():
            hello({"mod": other("mod", nm - 1)})

        @pl.when(jnp.logical_not(last))
        def _():
            hello({"mod": other("mod", 1)})

        for d in range(1, nf):
            hello({"frm": other("frm", d)})
        for b in bits:
            hello({"ori": flip(o, b)})

    barrier = pltpu.get_barrier_semaphore()
    greet(barrier)
    for copy in loads:
        copy.wait()

    def count_row(i):
        return counts[pl.ds(i, fr, stride=rows), :].astype(f32)

    for i in range(PASSES):
        halo_s[0, i] = count_row(i).astype(bf16)
        halo_s[1, i] = count_row(rows - PASSES + i).astype(bf16)
    pl.semaphore_wait(barrier, links)

    def part(g):
        return pl.ds(g * gsz, gsz)

    def halo_copy(side, g):
        return pltpu.make_async_remote_copy(
            src_ref=halo_s.at[side, :, part(g), :],
            dst_ref=halo_r.at[1 - side, :, part(g), :],
            send_sem=hs_sem.at[side, g],
            recv_sem=hr_sem.at[1 - side, g],
            device_id={"mod": other("mod", nm - 1 if side == 0 else 1)},
            device_id_type=MESH,
        )

    @pl.when(jnp.logical_not(first))
    def _():
        for g in range(groups):
            halo_copy(0, g).start()

    @pl.when(jnp.logical_not(last))
    def _():
        for g in range(groups):
            halo_copy(1, g).start()

    def load_row(i, carry):
        row = count_row(i) * SCALE
        for g in range(groups):
            inten[g, PASSES + i] = row[g * gsz : (g + 1) * gsz]
        return carry

    lax.fori_loop(0, rows, load_row, 0)
    inten[:, pl.ds(high, STRIDE_ROWS)] = jnp.zeros((groups, STRIDE_ROWS, gsz, lanes), f32)
    slope[pl.ds(high, STRIDE_ROWS)] = jnp.zeros((STRIDE_ROWS, gsz, 2 * lanes), f32)
    if rounds:
        greet(know.at[0])
    row_of = lax.rem(lax.broadcasted_iota(jnp.int32, (2 * lanes, 2 * lanes), 0), lanes)
    col_of = lax.broadcasted_iota(jnp.int32, (2 * lanes, 2 * lanes), 1)
    here = lax.rem(col_of, lanes)
    beside = here + jnp.where(col_of < lanes, 1, -1)
    shifts = (
        jnp.where(row_of == beside, 1.0, 0.0) - jnp.where(row_of == here, 1.0, 0.0)
    ).astype(bf16)

    def slice_chunk(c):
        code_copy(c).wait()
        base = c * (SLICE_CHUNK * band)
        acc = jnp.zeros((SLICE_CHUNK, lanes), f32)
        for s in range(band):
            raw = codes_v[pl.ds(base + s, SLICE_CHUNK, stride=band), :]
            value = (LOG_FLOOR + raw.astype(f32) * CODE_STEP).astype(bf16)
            logs[pl.ds(c * SLICE_CHUNK, SLICE_CHUNK), pl.ds(s * lanes, lanes)] = value
            weight = mask[pl.ds(f * band + s, 1), :].astype(f32)
            acc = acc + jnp.exp(value.astype(f32)) * weight
        totals[:, pl.ds(c * SLICE_CHUNK, SLICE_CHUNK)] = jnp.sum(acc.T, axis=0, keepdims=True)

    def halo_in(g):
        @pl.when(first)
        def _():
            inten[g, pl.ds(0, PASSES)] = jnp.zeros((PASSES, gsz, lanes), f32)

        @pl.when(jnp.logical_not(first))
        def _():
            halo_copy(1, g).wait_recv()
            inten[g, pl.ds(0, PASSES)] = halo_r[0, :, part(g), :].astype(f32) * SCALE
            halo_copy(0, g).wait_send()

        @pl.when(last)
        def _():
            inten[g, pl.ds(PASSES + rows, PASSES)] = jnp.zeros((PASSES, gsz, lanes), f32)

        @pl.when(jnp.logical_not(last))
        def _():
            halo_copy(0, g).wait_recv()
            inten[g, pl.ds(PASSES + rows, PASSES)] = (
                halo_r[1, :, part(g), :].astype(f32) * SCALE
            )
            halo_copy(1, g).wait_send()

    def keep(i, value):
        top = value.astype(bf16)
        split[i, :, pl.ds(0, lanes)] = top
        split[i, :, pl.ds(lanes, lanes)] = (value - top.astype(f32)).astype(bf16)

    def diffuse(g):
        halo_in(g)

        def keep_row(i, carry):
            keep(i, inten[g, i])
            return carry

        lax.fori_loop(0, high, keep_row, 0)

        def one_pass(p, carry):
            slope[pl.ds(0, high)] = lax.dot_general(
                split[pl.ds(0, high)].reshape(high * gsz, 2 * lanes), shifts,
                (((1,), (0,)), ((), ())), preferred_element_type=f32,
            ).reshape(high, gsz, 2 * lanes)
            low = jnp.where(first, PASSES, p + 1)
            top = jnp.where(last, PASSES + rows, high - 1 - p)
            c = inten[g, low]
            before = flux(c - inten[g, low - 1])

            def some_rows(k, state):
                c, before = state
                i = low + STRIDE_ROWS * k
                below = [inten[g, i + r + 1] for r in range(STRIDE_ROWS)]
                fresh = []
                for r in range(STRIDE_ROWS):
                    after = flux(below[r] - c)
                    side = flux(slope[i + r, :, pl.ds(0, lanes)]) + flux(
                        slope[i + r, :, pl.ds(lanes, lanes)]
                    )
                    fresh.append(c + ((after - before) + side))
                    c, before = below[r], after
                for r in range(STRIDE_ROWS):
                    inten[g, i + r] = fresh[r]
                    keep(i + r, fresh[r])
                return c, before

            trips = (top - low + STRIDE_ROWS - 1) // STRIDE_ROWS
            lax.fori_loop(0, trips, some_rows, (c, before))
            edge = inten[g, PASSES + rows]
            inten[g, PASSES + rows] = jnp.where(last, 0.0, edge)
            return carry

        lax.fori_loop(0, PASSES, one_pass, 0)
        for i in range(rows):
            good = mask[i : i + 1, :].astype(f32) * (1.0 / SCALE)
            band_s[
                pl.ds((i // band) * fr + g * gsz, gsz), pl.ds((i % band) * lanes, lanes)
            ] = (inten[g, PASSES + i] * good).astype(bf16)

    def slot(ff, oo, g):
        return frames.at[pl.ds(((g * nf + ff) * no + oo) * gsz, gsz)]

    pending = []
    count = [0]

    def arrived(ff, oo, g):
        pltpu.make_async_remote_copy(
            src_ref=slot(ff, oo, g), dst_ref=slot(ff, oo, g),
            send_sem=gs_sem.at[0], recv_sem=gr_sem.at[ff * no + oo, g],
            device_id={"ori": other("ori", 1)}, device_id_type=MESH,
        ).wait_recv()

    def send(src, ff, oo, g, target):
        copy = pltpu.make_async_remote_copy(
            src_ref=src, dst_ref=slot(ff, oo, g),
            send_sem=gs_sem.at[count[0]], recv_sem=gr_sem.at[ff * no + oo, g],
            device_id=target, device_id_type=MESH,
        )
        count[0] += 1
        copy.start()
        pending.append(copy)

    def banded(ff, g):
        return band_s.at[pl.ds(ff * fr + g * gsz, gsz)]

    held = [[o]]
    for b in bits:
        held.append(held[-1] + [flip(h, b) for h in held[-1]])

    def first_hop(g):
        for d in range(1, nf):
            fd = other("frm", d)
            send(banded(fd, g), f, o, g, {"frm": fd})
        send(banded(f, g), f, o, g, {"ori": flip(o, bits[0])})
        own = pltpu.make_async_copy(banded(f, g), slot(f, o, g), own_sem.at[g])
        own.start()
        own.wait()

    def second_hop(g):
        for d in range(1, nf):
            fd = other("frm", d)
            arrived(fd, o, g)
            send(slot(fd, o, g), fd, o, g, {"ori": flip(o, bits[0])})

    def later_hop(k, g):
        for d in range(nf):
            for h in held[k][len(held[k]) // 2 :]:
                arrived(other("frm", d), h, g)
        if k < hops:
            for d in range(nf):
                for h in held[k]:
                    send(slot(other("frm", d), h, g), other("frm", d), h, g, {"ori": flip(o, bits[k])})

    def mine(ff):
        return pl.ds(pl.multiple_of(ff * gg, gg), gg)

    def columns(t):
        return pl.ds(t * TILE, TILE)

    def sent_columns(t):
        return pl.ds(0, lanes + TILE) if t == 0 else pl.ds(lanes + t * TILE, TILE)

    def x_copy(src_f, dst_f, g, t, n):
        return pltpu.make_async_remote_copy(
            src_ref=xs.at[g, dst_f, :, sent_columns(t)],
            dst_ref=xr.at[g, src_f, :, sent_columns(t)],
            send_sem=xs_sem.at[g, n, t], recv_sem=xr_sem.at[g, src_f, t],
            device_id={"frm": dst_f}, device_id_type=MESH,
        )

    def multiply(g, t):
        value = lax.dot_general(
            frames[pl.ds(g * nf * gg, nf * gg), :],
            logs[columns(t), :],
            (((1,), (1,)), ((), ())),
            preferred_element_type=f32,
        ) - totals[:, columns(t)]
        cross[g, :, columns(t)] = value
        if t == 0:
            mean = jnp.mean(value, axis=1, keepdims=True).astype(bf16).astype(f32)
            centre[g] = jnp.broadcast_to(mean, (nf * gg, lanes))
        for d in range(1, nf):
            fd = other("frm", d)
            middle = centre[g, mine(fd), :]
            if t == 0:
                xs[g, fd, :, pl.ds(0, lanes)] = middle.astype(bf16)
            for j in range(TILE // lanes):
                at = t * TILE + j * lanes
                xs[g, fd, :, pl.ds(lanes + at, lanes)] = (
                    cross[g, mine(fd), pl.ds(at, lanes)] - middle
                ).astype(bf16)
            copy = x_copy(f, fd, g, t, d)
            copy.start()
            pending.append(copy)

    def z_copy(src_m, dst_m, g, t, n):
        return pltpu.make_async_remote_copy(
            src_ref=zs.at[g, pl.ds(pl.multiple_of(dst_m * sg, sg), sg), sent_columns(t)],
            dst_ref=zr.at[g, src_m, :, sent_columns(t)],
            send_sem=zs_sem.at[g, n, t], recv_sem=zr_sem.at[g, src_m, t],
            device_id={"mod": dst_m}, device_id_type=MESH,
        )

    def reduce_frm(g, t):
        for d in range(1, nf):
            fd = other("frm", d)
            x_copy(fd, f, g, t, 0).wait_recv()
        parts = [(xr, other("frm", d)) for d in range(1, nf)]
        mids = [r[g, i, :, pl.ds(0, lanes)].astype(f32) for r, i in parts]
        middle = sum(mids, centre[g, mine(f), :]).astype(bf16).astype(f32)
        if t == 0:
            zs[g, :, pl.ds(0, lanes)] = middle.astype(bf16)
        for j in range(TILE // lanes):
            at = t * TILE + j * lanes
            value = cross[g, mine(f), pl.ds(at, lanes)]
            for (r, i), mid in zip(parts, mids):
                value = value + (r[g, i, :, pl.ds(lanes + at, lanes)].astype(f32) + mid)
            cross[g, mine(f), pl.ds(at, lanes)] = value
            zs[g, :, pl.ds(lanes + at, lanes)] = (value - middle).astype(bf16)
        for d in range(1, nm):
            copy = z_copy(m, other("mod", d), g, t, d)
            copy.start()
            pending.append(copy)

    wide = lax.broadcasted_iota(jnp.int32, (sg, 128), 1)

    def t_copy(src_o, dst_o, g, n):
        return pltpu.make_async_remote_copy(
            src_ref=stat_s.at[g], dst_ref=stat_r.at[g, src_o],
            send_sem=ts_sem.at[g, n], recv_sem=tr_sem.at[g, src_o],
            device_id={"ori": dst_o}, device_id_type=MESH,
        )

    def reduce_mod(g):
        for t in range(tiles):
            for d in range(1, nm):
                z_copy(other("mod", d), m, g, t, 0).wait_recv()
        at = pl.ds(pl.multiple_of(f * gg + m * sg, sg), sg)
        value = cross[g, at, :]
        for d in range(1, nm):
            md = other("mod", d)
            value = value + (
                zr[g, md, :, pl.ds(lanes, orient)].astype(f32) + zr[g, md, :, pl.ds(0, 1)].astype(f32)
            )
        value = value * (1.0 / math.sqrt(rows * nm * lanes))
        score[g] = value
        peak = jnp.max(value, axis=1, keepdims=True)
        mass = jnp.sum(jnp.exp(value - peak), axis=1, keepdims=True)
        stat_s[g] = jnp.where(wide < 64, peak, mass)
        for d in range(1, no):
            copy = t_copy(o, other("ori", d), g, d)
            copy.start()
            pending.append(copy)

    def finish(g):
        got = [stat_s[g]]
        for d in range(1, no):
            od = other("ori", d)
            t_copy(od, o, g, 0).wait_recv()
            got.append(stat_r[g, od])
        peaks, masses = [s[:, 0:1] for s in got], [s[:, 64:65] for s in got]
        top = functools.reduce(jnp.maximum, peaks)
        weight = sum(s * jnp.exp(p - top) for p, s in zip(peaks, masses))
        value = score[g] - (top + jnp.log(weight))
        blocks = 1 if groups == 1 else no // nm
        span = sg // blocks
        for s in range(blocks):
            out[pl.ds(s * fr + g * gsz, span), :] = value[s * span : (s + 1) * span, :]

    def knowing(r):
        pl.semaphore_wait(know.at[r], links)
        if r + 1 < rounds:
            greet(know.at[r + 1])

    early = chunks // 2
    tasks = []

    def task(when, call, *args):
        tasks.append((when, len(tasks), call, args))

    for r in range(rounds):
        task(0.3 + 0.1 * r, knowing, r)
    for c in range(chunks):
        task(-1.0 if c < early else 0.6 + (1.0 if 4 * c >= 3 * chunks else 0.0), slice_chunk, c)
    for g in range(groups):
        task(g, diffuse, g)
        task(g + 0.1, first_hop, g)
        task(g + 1.2, second_hop, g)
        for k in range(1, hops):
            task(g + 2.2 + 0.5 * (k - 1), later_hop, k, g)
        task(g + 2.3 + 0.5 * (hops - 2), later_hop, hops, g)
        for t in range(tiles):
            task(g + 2.4 + 0.5 * (hops - 2), multiply, g, t)
        for t in range(tiles):
            task(g + 3.3 + 0.5 * (hops - 2), reduce_frm, g, t)
        task(g + 4.2 + 0.5 * (hops - 2), reduce_mod, g)
        task(g + 4.9 + 0.5 * (hops - 2), finish, g)
    for _, _, call, args in sorted(tasks, key=lambda entry: entry[:2]):
        call(*args)
    for copy in pending:
        copy.wait_send()


def body(counts, slice_codes, pixel_mask):
    nm, nf, no = (lax.axis_size(a) for a in ("mod", "frm", "ori"))
    fr, rows, lanes = counts.shape
    orient, band, _ = slice_codes.shape
    group = no * fr
    share = group // nm
    depth = band * lanes
    high = rows + 2 * PASSES
    groups = group_count(nm, no, fr)
    gg = group // groups
    sg = gg // nm
    tiles = orient // TILE
    dims = (nm, nf, no, fr, rows, orient, band, groups)
    dma = pltpu.SemaphoreType.DMA
    f32, bf16 = jnp.float32, jnp.bfloat16
    result = pl.pallas_call(
        functools.partial(kernel, dims),
        out_shape=pltpu.VMEM((share, orient), f32),
        in_specs=[pl.BlockSpec(memory_space=pl.ANY)] * 3,
        scratch_shapes=[
            pltpu.VMEM((fr * rows, lanes), jnp.int32),
            pltpu.VMEM((rows, lanes), jnp.int32),
            pltpu.VMEM((orient * band, lanes), jnp.int32),
            pltpu.VMEM((orient, depth), bf16),
            pltpu.VMEM((groups, high + STRIDE_ROWS, fr // groups, lanes), f32),
            pltpu.VMEM((2, PASSES, fr, lanes), bf16),
            pltpu.VMEM((2, PASSES, fr, lanes), bf16),
            pltpu.VMEM((nf * fr, depth), bf16),
            pltpu.VMEM((nf * group, depth), bf16),
            pltpu.VMEM((groups, nf * gg, orient), f32),
            pltpu.VMEM((groups, nf * gg, lanes), f32),
            pltpu.VMEM((groups, nf, gg, lanes + orient), bf16),
            pltpu.VMEM((groups, nf, gg, lanes + orient), bf16),
            pltpu.VMEM((groups, gg, lanes + orient), bf16),
            pltpu.VMEM((groups, nm, sg, lanes + orient), bf16),
            pltpu.VMEM((groups, sg, orient), f32),
            pltpu.VMEM((groups, sg, 128), f32),
            pltpu.VMEM((groups, no, sg, 128), f32),
            pltpu.VMEM((1, orient), f32),
            pltpu.VMEM((high + STRIDE_ROWS, fr // groups, 2 * lanes), bf16),
            pltpu.VMEM((high + STRIDE_ROWS, fr // groups, 2 * lanes), f32),
            dma((2,)),
            pltpu.SemaphoreType.REGULAR((max(nm, no),)),
            dma((orient // SLICE_CHUNK,)),
            dma((2, groups)),
            dma((2, groups)),
            dma((groups,)),
            dma((groups * nf * (no + 1),)),
            dma((nf * no, groups)),
            dma((groups, nf, tiles)),
            dma((groups, nf, tiles)),
            dma((groups, nm, tiles)),
            dma((groups, nm, tiles)),
            dma((groups, no)),
            dma((groups, no)),
        ],
        compiler_params=pltpu.CompilerParams(collective_id=0, has_side_effects=True),
    )(counts.reshape(fr * rows, lanes), slice_codes.reshape(orient * band, lanes), pixel_mask)
    return result[None]


def solution(mesh):
    in_specs = (P(("frm", "ori"), "mod", None), P("ori", ("mod", "frm"), None), P("mod", None))
    out_specs = P("frm", "mod", "ori")
    return jax.shard_map(body, mesh=mesh, in_specs=in_specs, out_specs=out_specs, check_vma=False)
```

```python
import functools
import math

import jax
import jax.numpy as jnp
from jax import lax
from jax.experimental import pallas as pl
from jax.experimental.pallas import tpu as pltpu
from jax.sharding import PartitionSpec as P

PASSES = 8
TIME_STEP = 0.2
EDGE_SCALE = 2.0
LOG_FLOOR = -7.0
CODE_STEP = 1.0 / 256.0
GROUPS = 2
STRIDE_ROWS = 8
SLICE_CHUNK = 128
MESH = pl.DeviceIdType.MESH


SQUARE = EDGE_SCALE * EDGE_SCALE
DENOM = 1.0 / TIME_STEP
SCALE = math.sqrt(DENOM / SQUARE)
TILE = 256


def flux(v):
    return v / (DENOM + v * v)


def flip(h, b):
    return h + b - 2 * b * lax.rem(h // b, 2)


def group_count(nm, no, fr):
    count = 2
    while count > 1 and (nm > no or no % nm or fr % (16 * count)):
        count //= 2
    return count


def kernel(
    dims, counts_h, codes, mask_h, out,
    counts, mask, codes_v, logs, inten, halo_s, halo_r, band_s, frames, cross, centre, xs, xr, zs, zr,
    score, stat_s, stat_r, totals, split, slope,
    load_sem, know, code_sem, hs_sem, hr_sem, own_sem, gs_sem, gr_sem, xs_sem, xr_sem, zs_sem, zr_sem,
    ts_sem, tr_sem,
):
    nm, nf, no, fr, rows, orient, band, groups = dims
    m, f, o = lax.axis_index("mod"), lax.axis_index("frm"), lax.axis_index("ori")
    sizes = {"mod": (m, nm), "frm": (f, nf), "ori": (o, no)}
    lanes = counts.shape[1]
    high = rows + 2 * PASSES
    gsz = fr // groups
    gg = no * gsz
    sg = gg // nm
    chunks = orient // SLICE_CHUNK
    tiles = orient // TILE
    f32, bf16 = jnp.float32, jnp.bfloat16

    def other(axis, d):
        me, n = sizes[axis]
        return lax.rem(me + d, n)

    def code_copy(c):
        span = SLICE_CHUNK * band
        at = pl.ds(c * span, span)
        return pltpu.make_async_copy(codes.at[at], codes_v.at[at], code_sem.at[c])

    loads = [
        pltpu.make_async_copy(counts_h, counts, load_sem.at[0]),
        pltpu.make_async_copy(mask_h, mask, load_sem.at[1]),
    ]
    for copy in loads:
        copy.start()
    for c in range(chunks):
        code_copy(c).start()

    first, last = m == 0, m == nm - 1
    bits = []
    b = no // 2
    while b >= 1:
        bits.append(b)
        b //= 2
    hops = len(bits)
    links = nf - 1 + hops + jnp.where(first, 0, 1) + jnp.where(last, 0, 1)
    rounds = max(nm - 1, hops) - 1

    def greet(sem):
        def hello(target):
            pl.semaphore_signal(sem, inc=1, device_id=target, device_id_type=MESH)

        @pl.when(jnp.logical_not(first))
        def _():
            hello({"mod": other("mod", nm - 1)})

        @pl.when(jnp.logical_not(last))
        def _():
            hello({"mod": other("mod", 1)})

        for d in range(1, nf):
            hello({"frm": other("frm", d)})
        for b in bits:
            hello({"ori": flip(o, b)})

    barrier = pltpu.get_barrier_semaphore()
    greet(barrier)
    for copy in loads:
        copy.wait()

    def count_row(i):
        return counts[pl.ds(i, fr, stride=rows), :].astype(f32)

    for i in range(PASSES):
        halo_s[0, i] = count_row(i).astype(bf16)
        halo_s[1, i] = count_row(rows - PASSES + i).astype(bf16)
    pl.semaphore_wait(barrier, links)

    def part(g):
        return pl.ds(g * gsz, gsz)

    def halo_copy(side, g):
        return pltpu.make_async_remote_copy(
            src_ref=halo_s.at[side, :, part(g), :],
            dst_ref=halo_r.at[1 - side, :, part(g), :],
            send_sem=hs_sem.at[side, g],
            recv_sem=hr_sem.at[1 - side, g],
            device_id={"mod": other("mod", nm - 1 if side == 0 else 1)},
            device_id_type=MESH,
        )

    @pl.when(jnp.logical_not(first))
    def _():
        for g in range(groups):
            halo_copy(0, g).start()

    @pl.when(jnp.logical_not(last))
    def _():
        for g in range(groups):
            halo_copy(1, g).start()

    def load_row(i, carry):
        row = count_row(i) * SCALE
        for g in range(groups):
            inten[g, PASSES + i] = row[g * gsz : (g + 1) * gsz]
        return carry

    lax.fori_loop(0, rows, load_row, 0)
    inten[:, pl.ds(high, STRIDE_ROWS)] = jnp.zeros((groups, STRIDE_ROWS, gsz, lanes), f32)
    slope[pl.ds(high, STRIDE_ROWS)] = jnp.zeros((STRIDE_ROWS, gsz, 2 * lanes), f32)
    if rounds:
        greet(know.at[0])
    row_of = lax.rem(lax.broadcasted_iota(jnp.int32, (2 * lanes, 2 * lanes), 0), lanes)
    col_of = lax.broadcasted_iota(jnp.int32, (2 * lanes, 2 * lanes), 1)
    here = lax.rem(col_of, lanes)
    beside = here + jnp.where(col_of < lanes, 1, -1)
    shifts = (
        jnp.where(row_of == beside, 1.0, 0.0) - jnp.where(row_of == here, 1.0, 0.0)
    ).astype(bf16)

    def slice_chunk(c):
        code_copy(c).wait()
        base = c * (SLICE_CHUNK * band)
        acc = jnp.zeros((SLICE_CHUNK, lanes), f32)
        for s in range(band):
            raw = codes_v[pl.ds(base + s, SLICE_CHUNK, stride=band), :]
            value = (LOG_FLOOR + raw.astype(f32) * CODE_STEP).astype(bf16)
            logs[pl.ds(c * SLICE_CHUNK, SLICE_CHUNK), pl.ds(s * lanes, lanes)] = value
            weight = mask[pl.ds(f * band + s, 1), :].astype(f32)
            acc = acc + jnp.exp(value.astype(f32)) * weight
        totals[:, pl.ds(c * SLICE_CHUNK, SLICE_CHUNK)] = jnp.sum(acc.T, axis=0, keepdims=True)

    def halo_in(g):
        @pl.when(first)
        def _():
            inten[g, pl.ds(0, PASSES)] = jnp.zeros((PASSES, gsz, lanes), f32)

        @pl.when(jnp.logical_not(first))
        def _():
            halo_copy(1, g).wait_recv()
            inten[g, pl.ds(0, PASSES)] = halo_r[0, :, part(g), :].astype(f32) * SCALE
            halo_copy(0, g).wait_send()

        @pl.when(last)
        def _():
            inten[g, pl.ds(PASSES + rows, PASSES)] = jnp.zeros((PASSES, gsz, lanes), f32)

        @pl.when(jnp.logical_not(last))
        def _():
            halo_copy(0, g).wait_recv()
            inten[g, pl.ds(PASSES + rows, PASSES)] = (
                halo_r[1, :, part(g), :].astype(f32) * SCALE
            )
            halo_copy(1, g).wait_send()

    def keep(i, value):
        top = value.astype(bf16)
        split[i, :, pl.ds(0, lanes)] = top
        split[i, :, pl.ds(lanes, lanes)] = (value - top.astype(f32)).astype(bf16)

    def diffuse(g):
        halo_in(g)

        def keep_row(i, carry):
            keep(i, inten[g, i])
            return carry

        lax.fori_loop(0, high, keep_row, 0)

        def one_pass(p, carry):
            slope[pl.ds(0, high)] = lax.dot_general(
                split[pl.ds(0, high)].reshape(high * gsz, 2 * lanes), shifts,
                (((1,), (0,)), ((), ())), preferred_element_type=f32,
            ).reshape(high, gsz, 2 * lanes)
            low = jnp.where(first, PASSES, p + 1)
            top = jnp.where(last, PASSES + rows, high - 1 - p)
            c = inten[g, low]
            before = flux(c - inten[g, low - 1])

            def some_rows(k, state):
                c, before = state
                i = low + STRIDE_ROWS * k
                below = [inten[g, i + r + 1] for r in range(STRIDE_ROWS)]
                fresh = []
                for r in range(STRIDE_ROWS):
                    after = flux(below[r] - c)
                    side = flux(slope[i + r, :, pl.ds(0, lanes)]) + flux(
                        slope[i + r, :, pl.ds(lanes, lanes)]
                    )
                    fresh.append(c + ((after - before) + side))
                    c, before = below[r], after
                for r in range(STRIDE_ROWS):
                    inten[g, i + r] = fresh[r]
                    keep(i + r, fresh[r])
                return c, before

            trips = (top - low + STRIDE_ROWS - 1) // STRIDE_ROWS
            lax.fori_loop(0, trips, some_rows, (c, before))
            edge = inten[g, PASSES + rows]
            inten[g, PASSES + rows] = jnp.where(last, 0.0, edge)
            return carry

        lax.fori_loop(0, PASSES, one_pass, 0)
        for i in range(rows):
            good = mask[i : i + 1, :].astype(f32) * (1.0 / SCALE)
            band_s[
                pl.ds((i // band) * fr + g * gsz, gsz), pl.ds((i % band) * lanes, lanes)
            ] = (inten[g, PASSES + i] * good).astype(bf16)

    def slot(ff, oo, g):
        return frames.at[pl.ds(((g * nf + ff) * no + oo) * gsz, gsz)]

    pending = []
    count = [0]

    def arrived(ff, oo, g):
        pltpu.make_async_remote_copy(
            src_ref=slot(ff, oo, g), dst_ref=slot(ff, oo, g),
            send_sem=gs_sem.at[0], recv_sem=gr_sem.at[ff * no + oo, g],
            device_id={"ori": other("ori", 1)}, device_id_type=MESH,
        ).wait_recv()

    def send(src, ff, oo, g, target):
        copy = pltpu.make_async_remote_copy(
            src_ref=src, dst_ref=slot(ff, oo, g),
            send_sem=gs_sem.at[count[0]], recv_sem=gr_sem.at[ff * no + oo, g],
            device_id=target, device_id_type=MESH,
        )
        count[0] += 1
        copy.start()
        pending.append(copy)

    def banded(ff, g):
        return band_s.at[pl.ds(ff * fr + g * gsz, gsz)]

    held = [[o]]
    for b in bits:
        held.append(held[-1] + [flip(h, b) for h in held[-1]])

    def first_hop(g):
        for d in range(1, nf):
            fd = other("frm", d)
            send(banded(fd, g), f, o, g, {"frm": fd})
        send(banded(f, g), f, o, g, {"ori": flip(o, bits[0])})
        own = pltpu.make_async_copy(banded(f, g), slot(f, o, g), own_sem.at[g])
        own.start()
        own.wait()

    def second_hop(g):
        for d in range(1, nf):
            fd = other("frm", d)
            arrived(fd, o, g)
            send(slot(fd, o, g), fd, o, g, {"ori": flip(o, bits[0])})

    def later_hop(k, g):
        for d in range(nf):
            for h in held[k][len(held[k]) // 2 :]:
                arrived(other("frm", d), h, g)
        if k < hops:
            for d in range(nf):
                for h in held[k]:
                    send(slot(other("frm", d), h, g), other("frm", d), h, g, {"ori": flip(o, bits[k])})

    def mine(ff):
        return pl.ds(pl.multiple_of(ff * gg, gg), gg)

    def columns(t):
        return pl.ds(t * TILE, TILE)

    def sent_columns(t):
        return pl.ds(0, lanes + TILE) if t == 0 else pl.ds(lanes + t * TILE, TILE)

    def x_copy(src_f, dst_f, g, t, n):
        return pltpu.make_async_remote_copy(
            src_ref=xs.at[g, dst_f, :, sent_columns(t)],
            dst_ref=xr.at[g, src_f, :, sent_columns(t)],
            send_sem=xs_sem.at[g, n, t], recv_sem=xr_sem.at[g, src_f, t],
            device_id={"frm": dst_f}, device_id_type=MESH,
        )

    def multiply(g, t):
        value = lax.dot_general(
            frames[pl.ds(g * nf * gg, nf * gg), :],
            logs[columns(t), :],
            (((1,), (1,)), ((), ())),
            preferred_element_type=f32,
        ) - totals[:, columns(t)]
        cross[g, :, columns(t)] = value
        if t == 0:
            mean = jnp.mean(value, axis=1, keepdims=True).astype(bf16).astype(f32)
            centre[g] = jnp.broadcast_to(mean, (nf * gg, lanes))
        for d in range(1, nf):
            fd = other("frm", d)
            middle = centre[g, mine(fd), :]
            if t == 0:
                xs[g, fd, :, pl.ds(0, lanes)] = middle.astype(bf16)
            for j in range(TILE // lanes):
                at = t * TILE + j * lanes
                xs[g, fd, :, pl.ds(lanes + at, lanes)] = (
                    cross[g, mine(fd), pl.ds(at, lanes)] - middle
                ).astype(bf16)
            copy = x_copy(f, fd, g, t, d)
            copy.start()
            pending.append(copy)

    def z_copy(src_m, dst_m, g, t, n):
        return pltpu.make_async_remote_copy(
            src_ref=zs.at[g, pl.ds(pl.multiple_of(dst_m * sg, sg), sg), sent_columns(t)],
            dst_ref=zr.at[g, src_m, :, sent_columns(t)],
            send_sem=zs_sem.at[g, n, t], recv_sem=zr_sem.at[g, src_m, t],
            device_id={"mod": dst_m}, device_id_type=MESH,
        )

    def reduce_frm(g, t):
        for d in range(1, nf):
            fd = other("frm", d)
            x_copy(fd, f, g, t, 0).wait_recv()
        parts = [(xr, other("frm", d)) for d in range(1, nf)]
        mids = [r[g, i, :, pl.ds(0, lanes)].astype(f32) for r, i in parts]
        middle = sum(mids, centre[g, mine(f), :]).astype(bf16).astype(f32)
        if t == 0:
            zs[g, :, pl.ds(0, lanes)] = middle.astype(bf16)
        for j in range(TILE // lanes):
            at = t * TILE + j * lanes
            value = cross[g, mine(f), pl.ds(at, lanes)]
            for (r, i), mid in zip(parts, mids):
                value = value + (r[g, i, :, pl.ds(lanes + at, lanes)].astype(f32) + mid)
            cross[g, mine(f), pl.ds(at, lanes)] = value
            zs[g, :, pl.ds(lanes + at, lanes)] = (value - middle).astype(bf16)
        for d in range(1, nm):
            copy = z_copy(m, other("mod", d), g, t, d)
            copy.start()
            pending.append(copy)

    wide = lax.broadcasted_iota(jnp.int32, (sg, 128), 1)

    def t_copy(src_o, dst_o, g, n):
        return pltpu.make_async_remote_copy(
            src_ref=stat_s.at[g], dst_ref=stat_r.at[g, src_o],
            send_sem=ts_sem.at[g, n], recv_sem=tr_sem.at[g, src_o],
            device_id={"ori": dst_o}, device_id_type=MESH,
        )

    def reduce_mod(g):
        for t in range(tiles):
            for d in range(1, nm):
                z_copy(other("mod", d), m, g, t, 0).wait_recv()
        at = pl.ds(pl.multiple_of(f * gg + m * sg, sg), sg)
        value = cross[g, at, :]
        for d in range(1, nm):
            md = other("mod", d)
            value = value + (
                zr[g, md, :, pl.ds(lanes, orient)].astype(f32) + zr[g, md, :, pl.ds(0, 1)].astype(f32)
            )
        value = value * (1.0 / math.sqrt(rows * nm * lanes))
        score[g] = value
        peak = jnp.max(value, axis=1, keepdims=True)
        mass = jnp.sum(jnp.exp(value - peak), axis=1, keepdims=True)
        stat_s[g] = jnp.where(wide < 64, peak, mass)
        for d in range(1, no):
            copy = t_copy(o, other("ori", d), g, d)
            copy.start()
            pending.append(copy)

    def finish(g):
        got = [stat_s[g]]
        for d in range(1, no):
            od = other("ori", d)
            t_copy(od, o, g, 0).wait_recv()
            got.append(stat_r[g, od])
        peaks, masses = [s[:, 0:1] for s in got], [s[:, 64:65] for s in got]
        top = functools.reduce(jnp.maximum, peaks)
        weight = sum(s * jnp.exp(p - top) for p, s in zip(peaks, masses))
        value = score[g] - (top + jnp.log(weight))
        blocks = 1 if groups == 1 else no // nm
        span = sg // blocks
        for s in range(blocks):
            out[pl.ds(s * fr + g * gsz, span), :] = value[s * span : (s + 1) * span, :]

    def knowing(r):
        pl.semaphore_wait(know.at[r], links)
        if r + 1 < rounds:
            greet(know.at[r + 1])

    early = chunks // 2
    tasks = []

    def task(when, call, *args):
        tasks.append((when, len(tasks), call, args))

    for r in range(rounds):
        task(0.3 + 0.1 * r, knowing, r)
    for c in range(chunks):
        task(-1.0 if c < early else 0.6 + (1.0 if 4 * c >= 3 * chunks else 0.0), slice_chunk, c)
    for g in range(groups):
        task(g, diffuse, g)
        task(g + 0.1, first_hop, g)
        task(g + 1.2, second_hop, g)
        for k in range(1, hops):
            task(g + 2.2 + 0.5 * (k - 1), later_hop, k, g)
        task(g + 2.3 + 0.5 * (hops - 2), later_hop, hops, g)
        for t in range(tiles):
            task(g + 2.4 + 0.5 * (hops - 2), multiply, g, t)
        for t in range(tiles):
            task(g + 3.3 + 0.5 * (hops - 2), reduce_frm, g, t)
        task(g + 4.2 + 0.5 * (hops - 2), reduce_mod, g)
        task(g + 4.9 + 0.5 * (hops - 2), finish, g)
    for _, _, call, args in sorted(tasks, key=lambda entry: entry[:2]):
        call(*args)
    for copy in pending:
        copy.wait_send()


def body(counts, slice_codes, pixel_mask):
    nm, nf, no = (lax.axis_size(a) for a in ("mod", "frm", "ori"))
    fr, rows, lanes = counts.shape
    orient, band, _ = slice_codes.shape
    group = no * fr
    share = group // nm
    depth = band * lanes
    high = rows + 2 * PASSES
    groups = group_count(nm, no, fr)
    gg = group // groups
    sg = gg // nm
    tiles = orient // TILE
    dims = (nm, nf, no, fr, rows, orient, band, groups)
    dma = pltpu.SemaphoreType.DMA
    f32, bf16 = jnp.float32, jnp.bfloat16
    result = pl.pallas_call(
        functools.partial(kernel, dims),
        out_shape=pltpu.VMEM((share, orient), f32),
        in_specs=[pl.BlockSpec(memory_space=pl.ANY)] * 3,
        scratch_shapes=[
            pltpu.VMEM((fr * rows, lanes), jnp.int32),
            pltpu.VMEM((rows, lanes), jnp.int32),
            pltpu.VMEM((orient * band, lanes), jnp.int32),
            pltpu.VMEM((orient, depth), bf16),
            pltpu.VMEM((groups, high + STRIDE_ROWS, fr // groups, lanes), f32),
            pltpu.VMEM((2, PASSES, fr, lanes), bf16),
            pltpu.VMEM((2, PASSES, fr, lanes), bf16),
            pltpu.VMEM((nf * fr, depth), bf16),
            pltpu.VMEM((nf * group, depth), bf16),
            pltpu.VMEM((groups, nf * gg, orient), f32),
            pltpu.VMEM((groups, nf * gg, lanes), f32),
            pltpu.VMEM((groups, nf, gg, lanes + orient), bf16),
            pltpu.VMEM((groups, nf, gg, lanes + orient), bf16),
            pltpu.VMEM((groups, gg, lanes + orient), bf16),
            pltpu.VMEM((groups, nm, sg, lanes + orient), bf16),
            pltpu.VMEM((groups, sg, orient), f32),
            pltpu.VMEM((groups, sg, 128), f32),
            pltpu.VMEM((groups, no, sg, 128), f32),
            pltpu.VMEM((1, orient), f32),
            pltpu.VMEM((high + STRIDE_ROWS, fr // groups, 2 * lanes), bf16),
            pltpu.VMEM((high + STRIDE_ROWS, fr // groups, 2 * lanes), f32),
            dma((2,)),
            pltpu.SemaphoreType.REGULAR((max(nm, no),)),
            dma((orient // SLICE_CHUNK,)),
            dma((2, groups)),
            dma((2, groups)),
            dma((groups,)),
            dma((groups * nf * (no + 1),)),
            dma((nf * no, groups)),
            dma((groups, nf, tiles)),
            dma((groups, nf, tiles)),
            dma((groups, nm, tiles)),
            dma((groups, nm, tiles)),
            dma((groups, no)),
            dma((groups, no)),
        ],
        compiler_params=pltpu.CompilerParams(collective_id=0, has_side_effects=True),
    )(counts.reshape(fr * rows, lanes), slice_codes.reshape(orient * band, lanes), pixel_mask)
    return result[None]


def solution(mesh):
    in_specs = (P(("frm", "ori"), "mod", None), P("ori", ("mod", "frm"), None), P("mod", None))
    out_specs = P("frm", "mod", "ori")
    return jax.shard_map(body, mesh=mesh, in_specs=in_specs, out_specs=out_specs, check_vma=False)
```

```python
import functools
import math

import jax
import jax.numpy as jnp
from jax import lax
from jax.experimental import pallas as pl
from jax.experimental.pallas import tpu as pltpu
from jax.sharding import PartitionSpec as P

PASSES = 8
TIME_STEP = 0.2
EDGE_SCALE = 2.0
LOG_FLOOR = -7.0
CODE_STEP = 1.0 / 256.0
GROUPS = 2
STRIDE_ROWS = 8
SLICE_CHUNK = 128
MESH = pl.DeviceIdType.MESH


SQUARE = EDGE_SCALE * EDGE_SCALE
DENOM = 1.0 / TIME_STEP
SCALE = math.sqrt(DENOM / SQUARE)
TILE = 256


def flux(v):
    return v / (DENOM + v * v)


def flip(h, b):
    return h + b - 2 * b * lax.rem(h // b, 2)


def group_count(nm, no, fr):
    count = 2
    while count > 1 and (nm > no or no % nm or fr % (16 * count)):
        count //= 2
    return count


def kernel(
    dims, counts_h, codes, mask_h, out,
    counts, mask, codes_v, logs, inten, halo_s, halo_r, band_s, frames, cross, centre, xs, xr, zs, zr,
    score, stat_s, stat_r, totals, split, slope,
    load_sem, know, code_sem, hs_sem, hr_sem, own_sem, gs_sem, gr_sem, xs_sem, xr_sem, zs_sem, zr_sem,
    ts_sem, tr_sem,
):
    nm, nf, no, fr, rows, orient, band, groups = dims
    m, f, o = lax.axis_index("mod"), lax.axis_index("frm"), lax.axis_index("ori")
    sizes = {"mod": (m, nm), "frm": (f, nf), "ori": (o, no)}
    lanes = counts.shape[1]
    high = rows + 2 * PASSES
    gsz = fr // groups
    gg = no * gsz
    sg = gg // nm
    chunks = orient // SLICE_CHUNK
    tiles = orient // TILE
    f32, bf16 = jnp.float32, jnp.bfloat16

    def other(axis, d):
        me, n = sizes[axis]
        return lax.rem(me + d, n)

    def code_copy(c):
        span = SLICE_CHUNK * band
        at = pl.ds(c * span, span)
        return pltpu.make_async_copy(codes.at[at], codes_v.at[at], code_sem.at[c])

    loads = [
        pltpu.make_async_copy(counts_h, counts, load_sem.at[0]),
        pltpu.make_async_copy(mask_h, mask, load_sem.at[1]),
    ]
    for copy in loads:
        copy.start()
    for c in range(chunks):
        code_copy(c).start()

    first, last = m == 0, m == nm - 1
    bits = []
    b = no // 2
    while b >= 1:
        bits.append(b)
        b //= 2
    hops = len(bits)
    links = nf - 1 + hops + jnp.where(first, 0, 1) + jnp.where(last, 0, 1)
    rounds = max(nm - 1, hops) - 1

    def greet(sem):
        def hello(target):
            pl.semaphore_signal(sem, inc=1, device_id=target, device_id_type=MESH)

        @pl.when(jnp.logical_not(first))
        def _():
            hello({"mod": other("mod", nm - 1)})

        @pl.when(jnp.logical_not(last))
        def _():
            hello({"mod": other("mod", 1)})

        for d in range(1, nf):
            hello({"frm": other("frm", d)})
        for b in bits:
            hello({"ori": flip(o, b)})

    barrier = pltpu.get_barrier_semaphore()
    greet(barrier)
    for copy in loads:
        copy.wait()

    def count_row(i):
        return counts[pl.ds(i, fr, stride=rows), :].astype(f32)

    for i in range(PASSES):
        halo_s[0, i] = count_row(i).astype(bf16)
        halo_s[1, i] = count_row(rows - PASSES + i).astype(bf16)
    pl.semaphore_wait(barrier, links)

    def part(g):
        return pl.ds(g * gsz, gsz)

    def halo_copy(side, g):
        return pltpu.make_async_remote_copy(
            src_ref=halo_s.at[side, :, part(g), :],
            dst_ref=halo_r.at[1 - side, :, part(g), :],
            send_sem=hs_sem.at[side, g],
            recv_sem=hr_sem.at[1 - side, g],
            device_id={"mod": other("mod", nm - 1 if side == 0 else 1)},
            device_id_type=MESH,
        )

    @pl.when(jnp.logical_not(first))
    def _():
        for g in range(groups):
            halo_copy(0, g).start()

    @pl.when(jnp.logical_not(last))
    def _():
        for g in range(groups):
            halo_copy(1, g).start()

    def load_row(i, carry):
        row = count_row(i) * SCALE
        for g in range(groups):
            inten[g, PASSES + i] = row[g * gsz : (g + 1) * gsz]
        return carry

    lax.fori_loop(0, rows, load_row, 0)
    inten[:, pl.ds(high, STRIDE_ROWS)] = jnp.zeros((groups, STRIDE_ROWS, gsz, lanes), f32)
    slope[pl.ds(high, STRIDE_ROWS)] = jnp.zeros((STRIDE_ROWS, gsz, 2 * lanes), f32)
    if rounds:
        greet(know.at[0])
    row_of = lax.rem(lax.broadcasted_iota(jnp.int32, (2 * lanes, 2 * lanes), 0), lanes)
    col_of = lax.broadcasted_iota(jnp.int32, (2 * lanes, 2 * lanes), 1)
    here = lax.rem(col_of, lanes)
    beside = here + jnp.where(col_of < lanes, 1, -1)
    shifts = (
        jnp.where(row_of == beside, 1.0, 0.0) - jnp.where(row_of == here, 1.0, 0.0)
    ).astype(bf16)

    def slice_chunk(c):
        code_copy(c).wait()
        base = c * (SLICE_CHUNK * band)
        acc = jnp.zeros((SLICE_CHUNK, lanes), f32)
        for s in range(band):
            raw = codes_v[pl.ds(base + s, SLICE_CHUNK, stride=band), :]
            value = (LOG_FLOOR + raw.astype(f32) * CODE_STEP).astype(bf16)
            logs[pl.ds(c * SLICE_CHUNK, SLICE_CHUNK), pl.ds(s * lanes, lanes)] = value
            weight = mask[pl.ds(f * band + s, 1), :].astype(f32)
            acc = acc + jnp.exp(value.astype(f32)) * weight
        totals[:, pl.ds(c * SLICE_CHUNK, SLICE_CHUNK)] = jnp.sum(acc.T, axis=0, keepdims=True)

    def halo_in(g):
        @pl.when(first)
        def _():
            inten[g, pl.ds(0, PASSES)] = jnp.zeros((PASSES, gsz, lanes), f32)

        @pl.when(jnp.logical_not(first))
        def _():
            halo_copy(1, g).wait_recv()
            inten[g, pl.ds(0, PASSES)] = halo_r[0, :, part(g), :].astype(f32) * SCALE
            halo_copy(0, g).wait_send()

        @pl.when(last)
        def _():
            inten[g, pl.ds(PASSES + rows, PASSES)] = jnp.zeros((PASSES, gsz, lanes), f32)

        @pl.when(jnp.logical_not(last))
        def _():
            halo_copy(0, g).wait_recv()
            inten[g, pl.ds(PASSES + rows, PASSES)] = (
                halo_r[1, :, part(g), :].astype(f32) * SCALE
            )
            halo_copy(1, g).wait_send()

    def keep(i, value):
        top = value.astype(bf16)
        split[i, :, pl.ds(0, lanes)] = top
        split[i, :, pl.ds(lanes, lanes)] = (value - top.astype(f32)).astype(bf16)

    def diffuse(g):
        halo_in(g)

        def keep_row(i, carry):
            keep(i, inten[g, i])
            return carry

        lax.fori_loop(0, high, keep_row, 0)

        def one_pass(p, carry):
            slope[pl.ds(0, high)] = lax.dot_general(
                split[pl.ds(0, high)].reshape(high * gsz, 2 * lanes), shifts,
                (((1,), (0,)), ((), ())), preferred_element_type=f32,
            ).reshape(high, gsz, 2 * lanes)
            low = jnp.where(first, PASSES, p + 1)
            top = jnp.where(last, PASSES + rows, high - 1 - p)
            c = inten[g, low]
            before = flux(c - inten[g, low - 1])

            def some_rows(k, state):
                c, before = state
                i = low + STRIDE_ROWS * k
                below = [inten[g, i + r + 1] for r in range(STRIDE_ROWS)]
                fresh = []
                for r in range(STRIDE_ROWS):
                    after = flux(below[r] - c)
                    side = flux(slope[i + r, :, pl.ds(0, lanes)]) + flux(
                        slope[i + r, :, pl.ds(lanes, lanes)]
                    )
                    fresh.append(c + ((after - before) + side))
                    c, before = below[r], after
                for r in range(STRIDE_ROWS):
                    inten[g, i + r] = fresh[r]
                    keep(i + r, fresh[r])
                return c, before

            trips = (top - low + STRIDE_ROWS - 1) // STRIDE_ROWS
            lax.fori_loop(0, trips, some_rows, (c, before))
            edge = inten[g, PASSES + rows]
            inten[g, PASSES + rows] = jnp.where(last, 0.0, edge)
            return carry

        lax.fori_loop(0, PASSES, one_pass, 0)
        for i in range(rows):
            good = mask[i : i + 1, :].astype(f32) * (1.0 / SCALE)
            band_s[
                pl.ds((i // band) * fr + g * gsz, gsz), pl.ds((i % band) * lanes, lanes)
            ] = (inten[g, PASSES + i] * good).astype(bf16)

    def slot(ff, oo, g):
        return frames.at[pl.ds(((g * nf + ff) * no + oo) * gsz, gsz)]

    pending = []
    count = [0]

    def arrived(ff, oo, g):
        pltpu.make_async_remote_copy(
            src_ref=slot(ff, oo, g), dst_ref=slot(ff, oo, g),
            send_sem=gs_sem.at[0], recv_sem=gr_sem.at[ff * no + oo, g],
            device_id={"ori": other("ori", 1)}, device_id_type=MESH,
        ).wait_recv()

    def send(src, ff, oo, g, target):
        copy = pltpu.make_async_remote_copy(
            src_ref=src, dst_ref=slot(ff, oo, g),
            send_sem=gs_sem.at[count[0]], recv_sem=gr_sem.at[ff * no + oo, g],
            device_id=target, device_id_type=MESH,
        )
        count[0] += 1
        copy.start()
        pending.append(copy)

    def banded(ff, g):
        return band_s.at[pl.ds(ff * fr + g * gsz, gsz)]

    held = [[o]]
    for b in bits:
        held.append(held[-1] + [flip(h, b) for h in held[-1]])

    def first_hop(g):
        for d in range(1, nf):
            fd = other("frm", d)
            send(banded(fd, g), f, o, g, {"frm": fd})
        send(banded(f, g), f, o, g, {"ori": flip(o, bits[0])})
        own = pltpu.make_async_copy(banded(f, g), slot(f, o, g), own_sem.at[g])
        own.start()
        own.wait()

    def second_hop(g):
        for d in range(1, nf):
            fd = other("frm", d)
            arrived(fd, o, g)
            send(slot(fd, o, g), fd, o, g, {"ori": flip(o, bits[0])})

    def later_hop(k, g):
        for d in range(nf):
            for h in held[k][len(held[k]) // 2 :]:
                arrived(other("frm", d), h, g)
        if k < hops:
            for d in range(nf):
                for h in held[k]:
                    send(slot(other("frm", d), h, g), other("frm", d), h, g, {"ori": flip(o, bits[k])})

    def mine(ff):
        return pl.ds(pl.multiple_of(ff * gg, gg), gg)

    def columns(t):
        return pl.ds(t * TILE, TILE)

    def sent_columns(t):
        return pl.ds(0, lanes + TILE) if t == 0 else pl.ds(lanes + t * TILE, TILE)

    def x_copy(src_f, dst_f, g, t, n):
        return pltpu.make_async_remote_copy(
            src_ref=xs.at[g, dst_f, :, sent_columns(t)],
            dst_ref=xr.at[g, src_f, :, sent_columns(t)],
            send_sem=xs_sem.at[g, n, t], recv_sem=xr_sem.at[g, src_f, t],
            device_id={"frm": dst_f}, device_id_type=MESH,
        )

    def multiply(g, t):
        value = lax.dot_general(
            frames[pl.ds(g * nf * gg, nf * gg), :],
            logs[columns(t), :],
            (((1,), (1,)), ((), ())),
            preferred_element_type=f32,
        ) - totals[:, columns(t)]
        cross[g, :, columns(t)] = value
        if t == 0:
            mean = jnp.mean(value, axis=1, keepdims=True).astype(bf16).astype(f32)
            centre[g] = jnp.broadcast_to(mean, (nf * gg, lanes))
        for d in range(1, nf):
            fd = other("frm", d)
            middle = centre[g, mine(fd), :]
            if t == 0:
                xs[g, fd, :, pl.ds(0, lanes)] = middle.astype(bf16)
            for j in range(TILE // lanes):
                at = t * TILE + j * lanes
                xs[g, fd, :, pl.ds(lanes + at, lanes)] = (
                    cross[g, mine(fd), pl.ds(at, lanes)] - middle
                ).astype(bf16)
            copy = x_copy(f, fd, g, t, d)
            copy.start()
            pending.append(copy)

    def z_copy(src_m, dst_m, g, t, n):
        return pltpu.make_async_remote_copy(
            src_ref=zs.at[g, pl.ds(pl.multiple_of(dst_m * sg, sg), sg), sent_columns(t)],
            dst_ref=zr.at[g, src_m, :, sent_columns(t)],
            send_sem=zs_sem.at[g, n, t], recv_sem=zr_sem.at[g, src_m, t],
            device_id={"mod": dst_m}, device_id_type=MESH,
        )

    def reduce_frm(g, t):
        for d in range(1, nf):
            fd = other("frm", d)
            x_copy(fd, f, g, t, 0).wait_recv()
        parts = [(xr, other("frm", d)) for d in range(1, nf)]
        mids = [r[g, i, :, pl.ds(0, lanes)].astype(f32) for r, i in parts]
        middle = sum(mids, centre[g, mine(f), :]).astype(bf16).astype(f32)
        if t == 0:
            zs[g, :, pl.ds(0, lanes)] = middle.astype(bf16)
        for j in range(TILE // lanes):
            at = t * TILE + j * lanes
            value = cross[g, mine(f), pl.ds(at, lanes)]
            for (r, i), mid in zip(parts, mids):
                value = value + (r[g, i, :, pl.ds(lanes + at, lanes)].astype(f32) + mid)
            cross[g, mine(f), pl.ds(at, lanes)] = value
            zs[g, :, pl.ds(lanes + at, lanes)] = (value - middle).astype(bf16)
        for d in range(1, nm):
            copy = z_copy(m, other("mod", d), g, t, d)
            copy.start()
            pending.append(copy)

    wide = lax.broadcasted_iota(jnp.int32, (sg, 128), 1)

    def t_copy(src_o, dst_o, g, n):
        return pltpu.make_async_remote_copy(
            src_ref=stat_s.at[g], dst_ref=stat_r.at[g, src_o],
            send_sem=ts_sem.at[g, n], recv_sem=tr_sem.at[g, src_o],
            device_id={"ori": dst_o}, device_id_type=MESH,
        )

    def reduce_mod(g):
        for t in range(tiles):
            for d in range(1, nm):
                z_copy(other("mod", d), m, g, t, 0).wait_recv()
        at = pl.ds(pl.multiple_of(f * gg + m * sg, sg), sg)
        value = cross[g, at, :]
        for d in range(1, nm):
            md = other("mod", d)
            value = value + (
                zr[g, md, :, pl.ds(lanes, orient)].astype(f32) + zr[g, md, :, pl.ds(0, 1)].astype(f32)
            )
        value = value * (1.0 / math.sqrt(rows * nm * lanes))
        score[g] = value
        peak = jnp.max(value, axis=1, keepdims=True)
        mass = jnp.sum(jnp.exp(value - peak), axis=1, keepdims=True)
        stat_s[g] = jnp.where(wide < 64, peak, mass)
        for d in range(1, no):
            copy = t_copy(o, other("ori", d), g, d)
            copy.start()
            pending.append(copy)

    def finish(g):
        got = [stat_s[g]]
        for d in range(1, no):
            od = other("ori", d)
            t_copy(od, o, g, 0).wait_recv()
            got.append(stat_r[g, od])
        peaks, masses = [s[:, 0:1] for s in got], [s[:, 64:65] for s in got]
        top = functools.reduce(jnp.maximum, peaks)
        weight = sum(s * jnp.exp(p - top) for p, s in zip(peaks, masses))
        value = score[g] - (top + jnp.log(weight))
        blocks = 1 if groups == 1 else no // nm
        span = sg // blocks
        for s in range(blocks):
            out[pl.ds(s * fr + g * gsz, span), :] = value[s * span : (s + 1) * span, :]

    def knowing(r):
        pl.semaphore_wait(know.at[r], links)
        if r + 1 < rounds:
            greet(know.at[r + 1])

    early = chunks // 2
    tasks = []

    def task(when, call, *args):
        tasks.append((when, len(tasks), call, args))

    for r in range(rounds):
        task(0.3 + 0.1 * r, knowing, r)
    for c in range(chunks):
        task(-1.0 if c < early else 0.6 + (1.0 if 4 * c >= 3 * chunks else 0.0), slice_chunk, c)
    for g in range(groups):
        tail = g == groups - 1
        task(g, diffuse, g)
        task(g + 0.1, first_hop, g)
        task(g + 0.7, second_hop, g)
        for k in range(1, hops):
            task(g + (0.95 if tail else 1.15) + 0.01 * k, later_hop, k, g)
        task(g + (1.1 if tail else 1.8), later_hop, hops, g)
        for t in range(tiles):
            task(g + (1.15 if tail else 1.85), multiply, g, t)
        for t in range(tiles):
            task(g + (1.4 if tail else 2.05), reduce_frm, g, t)
        task(g + (1.6 if tail else 2.3), reduce_mod, g)
        task(g + (1.8 if tail else 2.5), finish, g)
    for _, _, call, args in sorted(tasks, key=lambda entry: entry[:2]):
        call(*args)
    for copy in pending:
        copy.wait_send()


def body(counts, slice_codes, pixel_mask):
    nm, nf, no = (lax.axis_size(a) for a in ("mod", "frm", "ori"))
    fr, rows, lanes = counts.shape
    orient, band, _ = slice_codes.shape
    group = no * fr
    share = group // nm
    depth = band * lanes
    high = rows + 2 * PASSES
    groups = group_count(nm, no, fr)
    gg = group // groups
    sg = gg // nm
    tiles = orient // TILE
    dims = (nm, nf, no, fr, rows, orient, band, groups)
    dma = pltpu.SemaphoreType.DMA
    f32, bf16 = jnp.float32, jnp.bfloat16
    result = pl.pallas_call(
        functools.partial(kernel, dims),
        out_shape=pltpu.VMEM((share, orient), f32),
        in_specs=[pl.BlockSpec(memory_space=pl.ANY)] * 3,
        scratch_shapes=[
            pltpu.VMEM((fr * rows, lanes), jnp.int32),
            pltpu.VMEM((rows, lanes), jnp.int32),
            pltpu.VMEM((orient * band, lanes), jnp.int32),
            pltpu.VMEM((orient, depth), bf16),
            pltpu.VMEM((groups, high + STRIDE_ROWS, fr // groups, lanes), f32),
            pltpu.VMEM((2, PASSES, fr, lanes), bf16),
            pltpu.VMEM((2, PASSES, fr, lanes), bf16),
            pltpu.VMEM((nf * fr, depth), bf16),
            pltpu.VMEM((nf * group, depth), bf16),
            pltpu.VMEM((groups, nf * gg, orient), f32),
            pltpu.VMEM((groups, nf * gg, lanes), f32),
            pltpu.VMEM((groups, nf, gg, lanes + orient), bf16),
            pltpu.VMEM((groups, nf, gg, lanes + orient), bf16),
            pltpu.VMEM((groups, gg, lanes + orient), bf16),
            pltpu.VMEM((groups, nm, sg, lanes + orient), bf16),
            pltpu.VMEM((groups, sg, orient), f32),
            pltpu.VMEM((groups, sg, 128), f32),
            pltpu.VMEM((groups, no, sg, 128), f32),
            pltpu.VMEM((1, orient), f32),
            pltpu.VMEM((high + STRIDE_ROWS, fr // groups, 2 * lanes), bf16),
            pltpu.VMEM((high + STRIDE_ROWS, fr // groups, 2 * lanes), f32),
            dma((2,)),
            pltpu.SemaphoreType.REGULAR((max(nm, no),)),
            dma((orient // SLICE_CHUNK,)),
            dma((2, groups)),
            dma((2, groups)),
            dma((groups,)),
            dma((groups * nf * (no + 1),)),
            dma((nf * no, groups)),
            dma((groups, nf, tiles)),
            dma((groups, nf, tiles)),
            dma((groups, nm, tiles)),
            dma((groups, nm, tiles)),
            dma((groups, no)),
            dma((groups, no)),
        ],
        compiler_params=pltpu.CompilerParams(collective_id=0, has_side_effects=True),
    )(counts.reshape(fr * rows, lanes), slice_codes.reshape(orient * band, lanes), pixel_mask)
    return result[None]


def solution(mesh):
    in_specs = (P(("frm", "ori"), "mod", None), P("ori", ("mod", "frm"), None), P("mod", None))
    out_specs = P("frm", "mod", "ori")
    return jax.shard_map(body, mesh=mesh, in_specs=in_specs, out_specs=out_specs, check_vma=False)
```
